32 devices in a mesh: groups: 2 (over x), sph: 16 (over z, y, core).
Axes of the slice: x: 2, y: 2, z: 4, core: 2. Of those that a mesh axis runs over, the one named last changes fastest.
Arguments:
- positions: float32 [512, 3], P('sph'), may hold values from -8 to 8
- wave_vectors: float32 [256, 3], replicated, may hold values from -5 to 5
- pattern: float32 [2, 448, 256], replicated, may hold values from -6 to 6
- dir_index: int32 [64], P('groups'), parts along dimension 0, may hold values from 0 to 255
- mie: float32 [2, 448, 512], P(None, None, 'sph'), may hold values from -0.9 to 0.9
- trans_table: bfloat16 [8, 2, 448, 448], replicated, may hold values from -0.1875 to 0.1875
- pair_route: int32 [1024, 1], P('sph'), may hold values from 0 to 15; in each aligned block of 64 rows (0 to 63, 64 to 127, ...) at most 8 rows name the same one
- pair_source: int32 [1024], P('sph'), may hold values from 0 to 15
- pair_target: int32 [1024], P('sph'), may hold values from 0 to 15
- pair_class: int32 [1024], P('sph'), may hold values from 0 to 7
Outputs:
- scattered: bfloat16 [896, 32768], P(None, ('groups', 'sph')), parts along dimension 1
- extinction: float32 [64], P('groups'), parts along dimension 0
The draws below stay inside these ranges and needn't reach their ends.
There are 2 independent parts, one for each index of `groups`. The reference program is written for one: setup_inputs(seed, part) draws one part's arguments, and reference() takes and returns one part's arrays. A program takes and returns all parts, laid end to end along the dimension named above; an argument that names none is the same for every part. Nothing has to cross between parts.
Inputs may be any that keep to these rules, and one draw needn't show every extreme that they name: `pair_route`: among the rows of one device no device is named by more than 8 pairs, and in every draw some device is named by exactly 8 of them.
All inputs are finite; a program needn't handle non-finite values.
Results may differ from the reference program's by a relative error of at most 0.0051.
Values may be sent and summed in bfloat16 or wider, within the bound.
A program may use at most 192 MiB of HBM per device.

```python
import math
import jax
import jax.numpy as jnp
import numpy as np
from jax import lax

MODES = 448
DIRS = 32
DIRTAB = 256
CLASSES = 8
BLOCK = 2
BLK_DEV = 16
PAIRS_DEV = 64
CAP = 8
SPHERES = 512
PAIRS = 1024
N_SPH = 16


def place_ends(drawn, key, smallest, high):
    extent = drawn.shape
    index_at = [jax.random.randint(jax.random.fold_in(key, axis), (), 0, extent[axis]) for axis in range(len(extent))]
    drawn = drawn.at[tuple(index_at)].set(smallest)
    longest = extent.index(max(extent))
    index_at[longest] = (index_at[longest] + 1) % extent[longest]
    return drawn.at[tuple(index_at)].set(high)


def shard_levels(stream_key, shape, shards, smallest, top_value):
    factor_of = 1.0
    for axis_at, shards_of in shards:
        heights = jax.random.uniform(jax.random.fold_in(jax.random.fold_in(stream_key, 6), axis_at), (shards_of,), jnp.float32, smallest / len(shards), top_value / len(shards))
        factor_of = factor_of * jnp.repeat(jnp.exp(heights), shape[axis_at] // shards_of).reshape((-1,) + (1,) * (len(shape) - 1 - axis_at))
    return factor_of


def shared_out(own_key, own, number, rows, number_of, top, bound, lean):
    order = jax.random.permutation(own_key, number_of)
    crowded, common = load_shares(number_of, rows * top, bound, lean, True), load_shares(number_of, rows * top, bound, lean, False)
    places = jnp.arange(number_of)

    def named(tallies, offset_by):
        used = int((tallies > 0).sum())
        fixed = max(1, used // 4)
        shifted = fixed + (places - fixed + offset_by * (used - fixed)) % max(1, number_of - fixed)
        return jnp.zeros((number_of,), jnp.int32).at[order[jnp.where(places < fixed, places, shifted)]].set(jnp.asarray(tallies, jnp.int32))

    tallies = jnp.where(number % 4 == 0, named(crowded, number // 4), named(common, number - number // 4 - 1))
    mixed = jax.random.permutation(jax.random.fold_in(own, 3), number_of)
    giver, sink = mixed[0:number_of // 2 * 2:2], mixed[1:number_of // 2 * 2:2]
    slack = jnp.minimum(tallies[giver] - 1, bound - tallies[sink]) // 2
    slack = jnp.where((giver == order[0]) | (sink == order[0]) | (tallies[sink] == 0), 0, jnp.maximum(slack, 0))
    shifted = jax.random.randint(jax.random.fold_in(own, 4), (number_of // 2,), 0, 1 << 20) % (slack + 1)
    tallies = tallies.at[giver].add(-shifted).at[sink].add(shifted)
    items = jnp.searchsorted(jnp.cumsum(tallies), jnp.arange(rows * top), side="right").astype(jnp.int32)
    table = items.reshape(top, rows).T
    table = table[jax.random.permutation(jax.random.fold_in(own, 1), rows)]
    offset_by = jax.random.randint(jax.random.fold_in(own, 2), (rows, 1), 0, top)
    return jnp.take_along_axis(table, (jnp.arange(top)[None, :] + offset_by) % top, axis=1)


def load_shares(count, total, bound, skew, full):
    portions = [(1 << 20) // math.isqrt(rank ** skew) + 1 for rank in range(1, count + 1)]
    largest = bound if full else min(bound, max(-(-total // count), total * portions[0] // sum(portions)))
    least = 1 if total - largest >= count - 1 else 0
    given, rest = [largest] + [least] * (count - 1), total - largest - least * (count - 1)
    while rest > 0:
        candidates = [i for i in range(1, count) if given[i] < largest] or [i for i in range(1, count) if given[i] < bound]
        pool, budget = sum([portions[i] for i in candidates]), rest
        for i in candidates:
            addition = min(bound - given[i], max(1, budget * portions[i] // pool), rest)
            given[i] = given[i] + addition
            rest = rest - addition
    return np.array(given)


def gaussian(key, shape, scale, most, kind=jnp.bfloat16):
    return jnp.clip(scale * jax.random.normal(key, shape, jnp.float32), -most, most).astype(kind)


def setup_inputs(seed: int = 0, part: int = 0) -> dict:
    key_list = jax.random.split(jax.random.key(seed), 11)
    part_splits = jax.random.split(jax.random.fold_in(key_list[10], part), 11)
    positions = jnp.clip(jax.random.uniform(key_list[0], (SPHERES, 3), jnp.float32, -8.0, 8.0) * shard_levels(key_list[0], (SPHERES, 3), ((0, 16),), -0.4, 0.0), -8.0, 8.0)
    wave_vectors = gaussian(key_list[1], (DIRTAB, 3), 1.0, 5.0, jnp.float32)
    pattern = gaussian(key_list[2], (2, MODES, DIRTAB), 1.0, 6.0, jnp.float32)
    dir_index = place_ends(jax.random.randint(part_splits[3], (DIRS,), 0, DIRTAB), jax.random.fold_in(part_splits[3], 1), 0, DIRTAB - 1).astype(jnp.int32)
    mie = jnp.clip(jax.random.uniform(key_list[4], (2, MODES, SPHERES), jnp.float32, -0.9, 0.9) * shard_levels(key_list[4], (2, MODES, SPHERES), ((2, 16),), -0.4, 0.0), -0.9, 0.9)
    trans_table = gaussian(key_list[5], (CLASSES, 2, MODES, MODES), (2 * MODES) ** -0.5, 0.1875)
    pair_route_keys = jax.random.split(jax.random.fold_in(key_list[6], 1), PAIRS // PAIRS_DEV)
    pair_route_turns = jax.random.permutation(jax.random.fold_in(key_list[6], 3), PAIRS // PAIRS_DEV)
    pair_route = jax.vmap(lambda own, number: shared_out(jax.random.fold_in(key_list[6], 2), own, number, PAIRS_DEV, N_SPH, 1, CAP, 2))(pair_route_keys, pair_route_turns).reshape((PAIRS, 1))
    pair_source = place_ends(jax.random.randint(key_list[7], (PAIRS,), 0, BLK_DEV), jax.random.fold_in(key_list[7], 1), 0, BLK_DEV - 1).astype(jnp.int32)
    pair_target = place_ends(jax.random.randint(key_list[8], (PAIRS,), 0, BLK_DEV), jax.random.fold_in(key_list[8], 1), 0, BLK_DEV - 1).astype(jnp.int32)
    pair_class = place_ends(jax.random.randint(key_list[9], (PAIRS,), 0, CLASSES), jax.random.fold_in(key_list[9], 1), 0, CLASSES - 1).astype(jnp.int32)
    return dict(positions=positions, wave_vectors=wave_vectors, pattern=pattern, dir_index=dir_index, mie=mie, trans_table=trans_table, pair_route=pair_route, pair_source=pair_source, pair_target=pair_target, pair_class=pair_class)


def reference(positions, wave_vectors, pattern, dir_index, mie, trans_table, pair_route, pair_source, pair_target, pair_class):
    directions = wave_vectors[dir_index]
    phases = positions[:, 0:1] * directions[None, :, 0] + positions[:, 1:2] * directions[None, :, 1] + positions[:, 2:3] * directions[None, :, 2]
    cosine = jnp.cos(phases)
    sine_part = jnp.sin(phases)
    chosen = pattern[:, :, dir_index]
    inc_real = cosine[None] * chosen[0][:, None, :] - sine_part[None] * chosen[1][:, None, :]
    inc_imag = cosine[None] * chosen[1][:, None, :] + sine_part[None] * chosen[0][:, None, :]
    mie_real = mie[0][:, :, None]
    mie_imag = mie[1][:, :, None]
    scat_real = mie_real * inc_real - mie_imag * inc_imag
    scat_imag = mie_real * inc_imag + mie_imag * inc_real
    coeffs = jnp.concatenate([scat_real, scat_imag], 0).astype(jnp.bfloat16)
    columns = BLOCK * DIRS
    block_count = SPHERES // BLOCK
    block_data = coeffs.reshape(2 * MODES, block_count, columns).transpose(1, 0, 2)
    owner = jnp.arange(PAIRS, dtype=jnp.int32) // PAIRS_DEV
    source_global = (owner * BLK_DEV + pair_source).astype(jnp.int32)
    target_global = (pair_route[:, 0] * BLK_DEV + pair_target).astype(jnp.int32)
    group_shape = (PAIRS // 8, 8)

    def add_group(field_sum, group_items):
        sources, targets, classes = group_items
        tables = trans_table[classes].astype(jnp.float32)
        values = block_data[sources].astype(jnp.float32)
        data_real = values[:, :MODES]
        data_imag = values[:, MODES:]
        highest = lax.Precision.HIGHEST
        part_real = jnp.einsum('kij,kjc->kic', tables[:, 0], data_real, precision=highest) - jnp.einsum('kij,kjc->kic', tables[:, 1], data_imag, precision=highest)
        part_imag = jnp.einsum('kij,kjc->kic', tables[:, 1], data_real, precision=highest) + jnp.einsum('kij,kjc->kic', tables[:, 0], data_imag, precision=highest)
        contribution = jnp.concatenate([part_real, part_imag], 1).astype(jnp.bfloat16)
        contribution = lax.optimization_barrier(contribution).astype(jnp.float32)
        return field_sum.at[targets].add(contribution), None

    initial = jnp.zeros((block_count, 2 * MODES, columns), jnp.float32)
    summed, unused = lax.scan(add_group, initial, (source_global.reshape(group_shape), target_global.reshape(group_shape), pair_class.astype(jnp.int32).reshape(group_shape)))
    summed = summed.transpose(1, 0, 2).reshape(2 * MODES, SPHERES, DIRS)
    total_real = inc_real + summed[:MODES]
    total_imag = inc_imag + summed[MODES:]
    out_real = mie_real * total_real - mie_imag * total_imag
    out_imag = mie_real * total_imag + mie_imag * total_real
    scattered = jnp.concatenate([out_real, out_imag], 0).reshape(2 * MODES, SPHERES * DIRS).astype(jnp.bfloat16)
    extinction = jnp.sum(inc_real * out_real + inc_imag * out_imag, axis=(0, 1))
    return (scattered, extinction)
```

```python
import functools

import jax
import jax.numpy as jnp
from jax import lax
from jax.experimental import pallas as pl
from jax.experimental.pallas import tpu as pltpu
from jax.sharding import PartitionSpec as P

BLOCK = 2
LANES = 128
HIGHEST = lax.Precision.HIGHEST


def round_up(value, unit):
    return -(-value // unit) * unit


def field_kernel(
    dims, cells, sources, table, mie_rows, phase_rows, pat_rows, pat_tile, mie, cosine, sine,
    scattered, ext, head, chain, matrix, mixed, acc,
):
    modes, wide, dirs, blocks, classes, step_blocks = dims
    step = pl.program_id(0)
    columns = BLOCK * dirs
    slots = chain.shape[0]

    @pl.when(step == 0)
    def _():
        def clear(cell, carry):
            head[cell] = -1
            return carry

        lax.fori_loop(0, blocks * classes, clear, 0)

        def link(slot, carry):
            cell = cells[slot]

            @pl.when(cell >= 0)
            def _():
                chain[slot] = head[cell]
                head[cell] = slot

            return carry

        lax.fori_loop(0, slots, link, 0)
        for kind in range(classes):
            at = kind * 2 * wide
            if wide > modes:
                for part in range(2):
                    end = at + (part + 1) * wide
                    matrix[:, end - LANES : end] = jnp.zeros((2 * modes, LANES), matrix.dtype)
            real, imag = table[kind, 0], table[kind, 1]
            matrix[:modes, at : at + modes] = real
            matrix[:modes, at + wide : at + wide + modes] = -imag
            matrix[modes:, at : at + modes] = imag
            matrix[modes:, at + wide : at + wide + modes] = real

    def product(slot):
        block = sources[slot]
        spread = jnp.broadcast_to(phase_rows[pl.ds(block, 1), :], (2 * columns, 2 * columns)).T
        reals, imags = [], []
        for j in range(BLOCK):
            row = mie_rows[pl.ds(block * BLOCK + j, 1), :]
            mr, mi = row[:, :wide], row[:, wide:]
            c = jnp.concatenate([spread[j * dirs : (j + 1) * dirs]] * (wide // LANES), 1)
            s = jnp.concatenate([spread[columns + j * dirs : columns + (j + 1) * dirs]] * (wide // LANES), 1)
            reals.append(c * mr - s * mi)
            imags.append(c * mi + s * mr)
        return jnp.concatenate(reals, 0), jnp.concatenate(imags, 0)

    def build(index, carry):
        kind, local = index // step_blocks, index % step_blocks
        first = head[kind * blocks + step * step_blocks + local]
        rows = pl.ds(pl.multiple_of(local * columns, columns), columns)
        left = pl.ds(pl.multiple_of(kind * 2 * wide, 2 * wide), wide)
        right = pl.ds(pl.multiple_of(kind * 2 * wide + wide, wide), wide)

        @pl.when(first < 0)
        def _():
            zero = jnp.zeros((columns, wide), mixed.dtype)
            mixed[rows, left] = zero
            mixed[rows, right] = zero

        @pl.when(first >= 0)
        def _():
            yr, yi = product(first)
            acc[0] = yr
            acc[1] = yi

            def more(slot):
                yr, yi = product(slot)
                acc[0] += yr
                acc[1] += yi
                return chain[slot]

            lax.while_loop(lambda slot: slot >= 0, more, chain[first])
            yr, yi = acc[0], acc[1]
            pr, pi = pat_rows[0], pat_rows[1]
            mixed[rows, left] = (yr * pr - yi * pi).astype(mixed.dtype)
            mixed[rows, right] = (yr * pi + yi * pr).astype(mixed.dtype)

        return carry

    lax.fori_loop(0, classes * step_blocks, build, 0)
    interaction = lax.dot_general(
        matrix[...], mixed[...], (((1,), (1,)), ((), ())), preferred_element_type=jnp.float32
    )
    width = step_blocks * columns
    per_step = width // dirs
    spheres = mie.shape[1]
    picked = (
        lax.broadcasted_iota(jnp.int32, (spheres, width), 0)
        == step * per_step + lax.broadcasted_iota(jnp.int32, (spheres, width), 1) // dirs
    ).astype(jnp.float32)
    spread_mie = jnp.dot(mie[...], picked, precision=HIGHEST, preferred_element_type=jnp.float32)
    mr, mi = spread_mie[:modes], spread_mie[modes:]
    c, s = cosine[...], sine[...]
    pr = jnp.concatenate([pat_tile[0]] * (width // LANES), 1)
    pi = jnp.concatenate([pat_tile[1]] * (width // LANES), 1)
    inc_r = c * pr - s * pi
    inc_i = c * pi + s * pr
    total_r = inc_r + interaction[:modes]
    total_i = inc_i + interaction[modes:]
    out_r = mr * total_r - mi * total_i
    out_i = mr * total_i + mi * total_r
    scattered[:modes, :] = out_r.astype(scattered.dtype)
    scattered[modes:, :] = out_i.astype(scattered.dtype)
    ext[...] = jnp.sum(inc_r * out_r + inc_i * out_i, axis=0, keepdims=True)


def shards(
    positions, wave_vectors, pattern, dir_index, mie, trans_table, pair_route, pair_source,
    pair_target, pair_class,
):
    modes = pattern.shape[1]
    wide = round_up(modes, LANES)
    spheres = positions.shape[0]
    dirs = dir_index.shape[0]
    columns = BLOCK * dirs
    blocks = spheres // BLOCK
    classes = trans_table.shape[0]
    devices = lax.axis_size("sph")
    me = lax.axis_index("sph")
    pair_count = pair_source.shape[0]
    capacity = max(2, 2 * pair_count // devices)
    slots = devices * capacity
    tables = wave_vectors.shape[0]

    select = (jnp.arange(tables, dtype=jnp.int32)[:, None] == dir_index[None, :]).astype(jnp.float32)
    k = jnp.dot(select.T, wave_vectors, precision=HIGHEST)
    phases = (
        positions[:, 0:1] * k[None, :, 0]
        + positions[:, 1:2] * k[None, :, 1]
        + positions[:, 2:3] * k[None, :, 2]
    )
    cosine, sine = jnp.cos(phases), jnp.sin(phases)
    phase_rows = jnp.concatenate(
        [cosine.reshape(blocks, columns), sine.reshape(blocks, columns)], 1
    )
    dest = pair_route[:, 0]
    order = jnp.arange(pair_count, dtype=jnp.int32)
    rank = jnp.sum(
        ((dest[:, None] == dest[None, :]) & (order[None, :] < order[:, None])).astype(jnp.int32), 1
    )
    slot_of = dest * capacity + rank
    match = slot_of[:, None] == jnp.arange(slots, dtype=jnp.int32)[None, :]
    cell_of = pair_class * blocks + pair_target
    source_of = me * blocks + pair_source
    slot_cell = jnp.sum(jnp.where(match, cell_of[:, None] + 1, 0), 0) - 1
    slot_source = jnp.sum(jnp.where(match, source_of[:, None], 0), 0)
    lists = jnp.stack([slot_cell, slot_source]).astype(jnp.int32)
    mie_rows = jnp.pad(jnp.transpose(mie, (2, 0, 1)), ((0, 0), (0, 0), (0, wide - modes)))
    mie_rows = mie_rows.reshape(spheres, 2 * wide)

    all_mie = lax.all_gather(mie_rows, "sph", axis=0, tiled=True)
    all_phases = lax.all_gather(phase_rows, "sph", axis=0, tiled=True)
    all_lists = lax.all_gather(lists, "sph", axis=0)
    mine = lax.dynamic_slice_in_dim(all_lists, me * capacity, capacity, 2)
    cells = mine[:, 0].reshape(slots)
    sources = mine[:, 1].reshape(slots)

    select_tile = jnp.concatenate([select] * (LANES // dirs), 1)
    pat_tile = jnp.einsum("cmt,td->cmd", pattern, select_tile, precision=HIGHEST)
    pat_rows = jnp.einsum("td,cmt->cdm", select, pattern, precision=HIGHEST)
    pat_rows = jnp.pad(jnp.concatenate([pat_rows] * BLOCK, 1), ((0, 0), (0, 0), (0, wide - modes)))

    step_blocks = 2 * LANES // columns
    width = step_blocks * columns
    once = pl.Buffered(1)

    def whole(array):
        zeros = (0,) * array.ndim
        return pl.BlockSpec(array.shape, lambda i, *_: zeros, pipeline_mode=once)

    flat_mie = mie.reshape(2 * modes, spheres)
    operands = (trans_table, all_mie, all_phases, pat_rows, pat_tile, flat_mie)
    line = pl.BlockSpec((1, width), lambda i, *_: (0, i))
    depth = classes * 2 * wide
    scattered, ext = pl.pallas_call(
        functools.partial(field_kernel, (modes, wide, dirs, blocks, classes, step_blocks)),
        grid_spec=pltpu.PrefetchScalarGridSpec(
            num_scalar_prefetch=2,
            grid=(blocks // step_blocks,),
            in_specs=[whole(x) for x in operands] + [line, line],
            out_specs=[pl.BlockSpec((2 * modes, width), lambda i, *_: (0, i)), line],
            scratch_shapes=[
                pltpu.SMEM((blocks * classes,), jnp.int32),
                pltpu.SMEM((slots,), jnp.int32),
                pltpu.VMEM((2 * modes, depth), jnp.bfloat16),
                pltpu.VMEM((width, depth), jnp.bfloat16),
                pltpu.VMEM((2, columns, wide), jnp.float32),
            ],
        ),
        out_shape=[
            jax.ShapeDtypeStruct((2 * modes, spheres * dirs), jnp.bfloat16),
            jax.ShapeDtypeStruct((1, spheres * dirs), jnp.float32),
        ],
        compiler_params=pltpu.CompilerParams(
            dimension_semantics=("arbitrary",), vmem_limit_bytes=60 * 1024 * 1024
        ),
        name="field",
    )(cells, sources, *operands, cosine.reshape(1, spheres * dirs), sine.reshape(1, spheres * dirs))
    extinction = lax.psum(jnp.sum(ext.reshape(spheres, dirs), 0), "sph")
    return (scattered, extinction)


def solution(mesh):
    placed = (
        P("sph", None), P(), P(), P("groups"), P(None, None, "sph"), P(),
        P("sph", None), P("sph"), P("sph"), P("sph"),
    )
    return jax.shard_map(
        shards,
        mesh=mesh,
        in_specs=placed,
        out_specs=(P(None, ("groups", "sph")), P("groups")),
        check_vma=False,
    )
```

```python
import functools

import jax
import jax.numpy as jnp
from jax import lax
from jax.experimental import pallas as pl
from jax.experimental.pallas import tpu as pltpu
from jax.sharding import PartitionSpec as P

BLOCK = 2
LANES = 128
HIGHEST = lax.Precision.HIGHEST


def round_up(value, unit):
    return -(-value // unit) * unit


MESH = pl.DeviceIdType.MESH


def gather_kernel(devices, mie, small, all_mie, all_small, send, recv, local):
    me = lax.axis_index("sph")
    chips = devices // 2
    chip, core = me // 2, me % 2
    other = chip * 2 + (1 - core)
    peers = [other] + [((chip + r) % chips) * 2 + core for r in range(1, chips)]
    barrier = pltpu.get_barrier_semaphore()
    for peer in peers:
        pl.semaphore_signal(barrier, inc=1, device_id={"sph": peer}, device_id_type=MESH)
    pl.semaphore_wait(barrier, chips)
    arrays = ((mie, all_mie), (small, all_small))

    def start(source, target, at, slot, peer):
        copy = pltpu.make_async_remote_copy(
            src_ref=source, dst_ref=target, send_sem=send.at[at, slot], recv_sem=recv.at[at, slot],
            device_id={"sph": peer}, device_id_type=MESH,
        )
        copy.start()
        return copy

    own = [pltpu.make_async_copy(a, out.at[me], local.at[i]) for i, (a, out) in enumerate(arrays)]
    first = {}
    for r in list(range(1, chips)) + [0]:
        for i, (a, out) in enumerate(arrays):
            first[i, r] = start(a, out.at[me], i, r, peers[r])
    for copy in own:
        copy.start()
    second = []
    for r in range(1, chips):
        origin = ((chip + chips - r) % chips) * 2 + core
        for i, (a, out) in enumerate(arrays):
            first[i, r].wait_recv()
            second.append(start(out.at[origin], out.at[origin], i, chips + r, other))
    for i in range(len(arrays)):
        first[i, 0].wait_recv()
    for copy in second:
        copy.wait_recv()
    for copy in own:
        copy.wait()
    for copy in list(first.values()) + second:
        copy.wait_send()


def gather_all(devices, mie_rows, small):
    spec = pl.BlockSpec(memory_space=pltpu.VMEM)
    anywhere = pl.BlockSpec(memory_space=pl.ANY)
    copies = pltpu.SemaphoreType.DMA((2, devices))
    return pl.pallas_call(
        functools.partial(gather_kernel, devices),
        out_shape=[jax.ShapeDtypeStruct((devices,) + a.shape, a.dtype) for a in (mie_rows, small)],
        in_specs=[spec, spec],
        out_specs=[anywhere, anywhere],
        scratch_shapes=[copies, copies, pltpu.SemaphoreType.DMA((2,))],
        compiler_params=pltpu.CompilerParams(collective_id=0, has_side_effects=True),
        name="gather",
    )(mie_rows, small)


def sum_kernel(devices, dirs, part, total, inbox, send, recv):
    me = lax.axis_index("sph")
    peers = [(me + r) % devices for r in range(1, devices)]
    barrier = pltpu.get_barrier_semaphore()
    for peer in peers:
        pl.semaphore_signal(barrier, inc=1, device_id={"sph": peer}, device_id_type=MESH)
    pl.semaphore_wait(barrier, devices - 1)
    copies = []
    for r, peer in enumerate(peers):
        copy = pltpu.make_async_remote_copy(
            src_ref=part, dst_ref=inbox.at[me], send_sem=send.at[r], recv_sem=recv.at[r],
            device_id={"sph": peer}, device_id_type=MESH,
        )
        copy.start()
        copies.append(copy)
    inbox[me] = part[...]
    for copy in copies:
        copy.wait_recv()
    row = jnp.sum(jnp.sum(inbox[...], 0), 0, keepdims=True)
    shift = LANES // 2
    while shift >= dirs:
        row = row + pltpu.roll(row, shift, 1)
        shift //= 2
    total[...] = row
    for copy in copies:
        copy.wait_send()


def sum_all(devices, dirs, part):
    spec = pl.BlockSpec(memory_space=pltpu.VMEM)
    copies = pltpu.SemaphoreType.DMA((devices,))
    return pl.pallas_call(
        functools.partial(sum_kernel, devices, dirs),
        out_shape=jax.ShapeDtypeStruct((1, LANES), jnp.float32),
        in_specs=[spec],
        out_specs=spec,
        scratch_shapes=[pltpu.VMEM((devices,) + part.shape, jnp.float32), copies, copies],
        compiler_params=pltpu.CompilerParams(collective_id=1, has_side_effects=True),
        name="extinction",
    )(part)


def field_kernel(
    dims, lists, table, mie_rows, phase_rows, pat_rows, pat_tile, mie, cosine, sine,
    scattered, ext, head, chain, phase_at, mie_at, matrix, mixed, acc,
):
    modes, wide, dirs, blocks, classes, step_blocks = dims
    step = pl.program_id(0)
    columns = BLOCK * dirs
    capacity = lists.shape[2]

    @pl.when(step == 0)
    def _():
        def clear(cell, carry):
            head[cell] = -1
            return carry

        lax.fori_loop(0, blocks * classes, clear, 0)

        def link(device, carry):
            for k in range(capacity):
                cell = lists[device, 0, k]
                slot = device * capacity + k

                @pl.when(cell >= 0)
                def _():
                    chain[slot] = head[cell]
                    head[cell] = slot
                    phase_at[slot] = lists[device, 1, k]
                    mie_at[slot] = lists[device, 2, k]

            return carry

        lax.fori_loop(0, lists.shape[0], link, 0)
        for kind in range(classes):
            at = kind * 2 * wide
            if wide > modes:
                for part in range(2):
                    end = at + (part + 1) * wide
                    matrix[:, end - LANES : end] = jnp.zeros((2 * modes, LANES), matrix.dtype)
            real, imag = table[kind, 0], table[kind, 1]
            matrix[:modes, at : at + modes] = real
            matrix[:modes, at + wide : at + wide + modes] = -imag
            matrix[modes:, at : at + modes] = imag
            matrix[modes:, at + wide : at + wide + modes] = real

    def product(slot):
        start = mie_at[slot]
        spread = jnp.broadcast_to(
            phase_rows[pl.ds(phase_at[slot], 1), :], (2 * columns, 2 * columns)
        ).T
        reals, imags = [], []
        for j in range(BLOCK):
            row = mie_rows[pl.ds(start + j, 1), :]
            mr, mi = row[:, :wide], row[:, wide:]
            c = jnp.concatenate([spread[j * dirs : (j + 1) * dirs]] * (wide // LANES), 1)
            s = jnp.concatenate([spread[columns + j * dirs : columns + (j + 1) * dirs]] * (wide // LANES), 1)
            reals.append(c * mr - s * mi)
            imags.append(c * mi + s * mr)
        return jnp.concatenate(reals, 0), jnp.concatenate(imags, 0)

    def build(index, carry):
        kind, local = index // step_blocks, index % step_blocks
        first = head[kind * blocks + step * step_blocks + local]
        rows = pl.ds(pl.multiple_of(local * columns, columns), columns)
        left = pl.ds(pl.multiple_of(kind * 2 * wide, 2 * wide), wide)
        right = pl.ds(pl.multiple_of(kind * 2 * wide + wide, wide), wide)

        @pl.when(first < 0)
        def _():
            zero = jnp.zeros((columns, wide), mixed.dtype)
            mixed[rows, left] = zero
            mixed[rows, right] = zero

        @pl.when(first >= 0)
        def _():
            yr, yi = product(first)
            acc[0] = yr
            acc[1] = yi

            def more(slot):
                yr, yi = product(slot)
                acc[0] += yr
                acc[1] += yi
                return chain[slot]

            lax.while_loop(lambda slot: slot >= 0, more, chain[first])
            yr, yi = acc[0], acc[1]
            pr, pi = pat_rows[0], pat_rows[1]
            mixed[rows, left] = (yr * pr - yi * pi).astype(mixed.dtype)
            mixed[rows, right] = (yr * pi + yi * pr).astype(mixed.dtype)

        return carry

    lax.fori_loop(0, classes * step_blocks, build, 0)
    interaction = lax.dot_general(
        matrix[...], mixed[...], (((1,), (1,)), ((), ())), preferred_element_type=jnp.float32
    )
    width = step_blocks * columns
    per_step = width // dirs
    spheres = mie.shape[1]
    picked = (
        lax.broadcasted_iota(jnp.int32, (spheres, width), 0)
        == step * per_step + lax.broadcasted_iota(jnp.int32, (spheres, width), 1) // dirs
    ).astype(jnp.float32)
    spread_mie = jnp.dot(mie[...], picked, precision=HIGHEST, preferred_element_type=jnp.float32)
    mr, mi = spread_mie[:modes], spread_mie[modes:]
    c, s = cosine[...], sine[...]
    pr = jnp.concatenate([pat_tile[0]] * (width // LANES), 1)
    pi = jnp.concatenate([pat_tile[1]] * (width // LANES), 1)
    inc_r = c * pr - s * pi
    inc_i = c * pi + s * pr
    total_r = inc_r + interaction[:modes]
    total_i = inc_i + interaction[modes:]
    out_r = mr * total_r - mi * total_i
    out_i = mr * total_i + mi * total_r
    scattered[:modes, :] = out_r.astype(scattered.dtype)
    scattered[modes:, :] = out_i.astype(scattered.dtype)
    terms = jnp.sum((inc_r * out_r + inc_i * out_i).reshape(modes // 8, 8, width), 0)
    part = sum(terms[:, at : at + LANES] for at in range(0, width, LANES))

    @pl.when(step == 0)
    def _():
        ext[...] = part

    @pl.when(step > 0)
    def _():
        ext[...] += part


def shards(
    positions, wave_vectors, pattern, dir_index, mie, trans_table, pair_route, pair_source,
    pair_target, pair_class,
):
    modes = pattern.shape[1]
    wide = round_up(modes, LANES)
    spheres = positions.shape[0]
    dirs = dir_index.shape[0]
    columns = BLOCK * dirs
    blocks = spheres // BLOCK
    classes = trans_table.shape[0]
    devices = lax.axis_size("sph")
    me = lax.axis_index("sph")
    pair_count = pair_source.shape[0]
    capacity = max(2, 2 * pair_count // devices)
    slots = devices * capacity
    tables = wave_vectors.shape[0]

    select = (jnp.arange(tables, dtype=jnp.int32)[:, None] == dir_index[None, :]).astype(jnp.float32)
    k = jnp.dot(select.T, wave_vectors, precision=HIGHEST)
    phases = (
        positions[:, 0:1] * k[None, :, 0]
        + positions[:, 1:2] * k[None, :, 1]
        + positions[:, 2:3] * k[None, :, 2]
    )
    cosine, sine = jnp.cos(phases), jnp.sin(phases)
    phase_rows = jnp.concatenate(
        [cosine.reshape(blocks, columns), sine.reshape(blocks, columns)], 1
    )
    dest = pair_route[:, 0]
    order = jnp.arange(pair_count, dtype=jnp.int32)
    rank = jnp.sum(
        ((dest[:, None] == dest[None, :]) & (order[None, :] < order[:, None])).astype(jnp.int32), 1
    )
    slot_of = dest * capacity + rank
    match = slot_of[:, None] == jnp.arange(slots, dtype=jnp.int32)[None, :]
    cell_of = pair_class * blocks + pair_target
    small_rows = round_up(blocks + 3, 8)
    entries = jnp.stack(
        [cell_of + 1, me * small_rows + pair_source, me * spheres + pair_source * BLOCK]
    )
    lists = jnp.sum(jnp.where(match[None], entries[:, :, None], 0), 1)
    lists = (lists - jnp.array([[1], [0], [0]], jnp.int32)).astype(jnp.float32)
    lists = jnp.pad(lists, ((0, small_rows - blocks - 3), (0, LANES - slots)))
    small = jnp.concatenate([phase_rows, lists], 0)
    mie_rows = jnp.pad(jnp.transpose(mie, (2, 0, 1)), ((0, 0), (0, 0), (0, wide - modes)))
    mie_rows = mie_rows.reshape(spheres, 2 * wide)

    all_mie, all_small = gather_all(devices, mie_rows, small)
    mine = lax.dynamic_slice_in_dim(all_small[:, blocks : blocks + 3], me * capacity, capacity, 2)
    mine = mine.astype(jnp.int32)
    all_mie = all_mie.reshape(devices * spheres, 2 * wide)
    all_small = all_small.reshape(devices * small_rows, LANES)

    select_tile = jnp.concatenate([select] * (LANES // dirs), 1)
    pat_tile = jnp.einsum("cmt,td->cmd", pattern, select_tile, precision=HIGHEST)
    pat_rows = jnp.einsum("td,cmt->cdm", select, pattern, precision=HIGHEST)
    pat_rows = jnp.pad(jnp.concatenate([pat_rows] * BLOCK, 1), ((0, 0), (0, 0), (0, wide - modes)))

    step_blocks = 2 * LANES // columns
    width = step_blocks * columns
    once = pl.Buffered(1)

    def whole(array):
        zeros = (0,) * array.ndim
        return pl.BlockSpec(array.shape, lambda i, *_: zeros, pipeline_mode=once)

    flat_mie = mie.reshape(2 * modes, spheres)
    operands = (trans_table, all_mie, all_small, pat_rows, pat_tile, flat_mie)
    line = pl.BlockSpec((1, width), lambda i, *_: (0, i))
    depth = classes * 2 * wide
    scattered, ext = pl.pallas_call(
        functools.partial(field_kernel, (modes, wide, dirs, blocks, classes, step_blocks)),
        grid_spec=pltpu.PrefetchScalarGridSpec(
            num_scalar_prefetch=1,
            grid=(blocks // step_blocks,),
            in_specs=[whole(x) for x in operands] + [line, line],
            out_specs=[
                pl.BlockSpec((2 * modes, width), lambda i, *_: (0, i)),
                pl.BlockSpec((8, LANES), lambda i, *_: (0, 0)),
            ],
            scratch_shapes=[
                pltpu.SMEM((blocks * classes,), jnp.int32),
                pltpu.SMEM((slots,), jnp.int32),
                pltpu.SMEM((slots,), jnp.int32),
                pltpu.SMEM((slots,), jnp.int32),
                pltpu.VMEM((2 * modes, depth), jnp.bfloat16),
                pltpu.VMEM((width, depth), jnp.bfloat16),
                pltpu.VMEM((2, columns, wide), jnp.float32),
            ],
        ),
        out_shape=[
            jax.ShapeDtypeStruct((2 * modes, spheres * dirs), jnp.bfloat16),
            jax.ShapeDtypeStruct((8, LANES), jnp.float32),
        ],
        compiler_params=pltpu.CompilerParams(
            dimension_semantics=("arbitrary",), vmem_limit_bytes=60 * 1024 * 1024
        ),
        name="field",
    )(mine, *operands, cosine.reshape(1, spheres * dirs), sine.reshape(1, spheres * dirs))
    return (scattered, sum_all(devices, dirs, ext)[0, :dirs])


def solution(mesh):
    placed = (
        P("sph", None), P(), P(), P("groups"), P(None, None, "sph"), P(),
        P("sph", None), P("sph"), P("sph"), P("sph"),
    )
    return jax.shard_map(
        shards,
        mesh=mesh,
        in_specs=placed,
        out_specs=(P(None, ("groups", "sph")), P("groups")),
        check_vma=False,
    )
```

```python
import functools

import jax
import jax.numpy as jnp
from jax import lax
from jax.experimental import pallas as pl
from jax.experimental.pallas import tpu as pltpu
from jax.sharding import PartitionSpec as P

BLOCK = 2
LANES = 128
HIGHEST = lax.Precision.HIGHEST


def round_up(value, unit):
    return -(-value // unit) * unit


MESH = pl.DeviceIdType.MESH


def gather_kernel(devices, mie, small, all_mie, all_small, send, recv, local):
    me = lax.axis_index("sph")
    chips = devices // 2
    chip, core = me // 2, me % 2
    other = chip * 2 + (1 - core)
    peers = [other] + [((chip + r) % chips) * 2 + core for r in range(1, chips)]
    barrier = pltpu.get_barrier_semaphore()
    for peer in peers:
        pl.semaphore_signal(barrier, inc=1, device_id={"sph": peer}, device_id_type=MESH)
    pl.semaphore_wait(barrier, chips)
    arrays = ((mie, all_mie), (small, all_small))

    def start(source, target, at, slot, peer):
        copy = pltpu.make_async_remote_copy(
            src_ref=source, dst_ref=target, send_sem=send.at[at, slot], recv_sem=recv.at[at, slot],
            device_id={"sph": peer}, device_id_type=MESH,
        )
        copy.start()
        return copy

    own = [pltpu.make_async_copy(a, out.at[me], local.at[i]) for i, (a, out) in enumerate(arrays)]
    first = {}
    for r in list(range(1, chips)) + [0]:
        for i, (a, out) in enumerate(arrays):
            first[i, r] = start(a, out.at[me], i, r, peers[r])
    for copy in own:
        copy.start()
    second = []
    for r in range(1, chips):
        origin = ((chip + chips - r) % chips) * 2 + core
        for i, (a, out) in enumerate(arrays):
            first[i, r].wait_recv()
            second.append(start(out.at[origin], out.at[origin], i, chips + r, other))
    for i in range(len(arrays)):
        first[i, 0].wait_recv()
    for copy in second:
        copy.wait_recv()
    for copy in own:
        copy.wait()
    for copy in list(first.values()) + second:
        copy.wait_send()


def gather_all(devices, mie_rows, small):
    spec = pl.BlockSpec(memory_space=pltpu.VMEM)
    anywhere = pl.BlockSpec(memory_space=pl.ANY)
    copies = pltpu.SemaphoreType.DMA((2, devices))
    return pl.pallas_call(
        functools.partial(gather_kernel, devices),
        out_shape=[jax.ShapeDtypeStruct((devices,) + a.shape, a.dtype) for a in (mie_rows, small)],
        in_specs=[spec, spec],
        out_specs=[anywhere, anywhere],
        scratch_shapes=[copies, copies, pltpu.SemaphoreType.DMA((2,))],
        compiler_params=pltpu.CompilerParams(collective_id=0, has_side_effects=True),
        name="gather",
    )(mie_rows, small)


def sum_kernel(devices, dirs, part, total, inbox, send, recv):
    me = lax.axis_index("sph")
    peers = [(me + r) % devices for r in range(1, devices)]
    barrier = pltpu.get_barrier_semaphore()
    for peer in peers:
        pl.semaphore_signal(barrier, inc=1, device_id={"sph": peer}, device_id_type=MESH)
    pl.semaphore_wait(barrier, devices - 1)
    copies = []
    for r, peer in enumerate(peers):
        copy = pltpu.make_async_remote_copy(
            src_ref=part, dst_ref=inbox.at[me], send_sem=send.at[r], recv_sem=recv.at[r],
            device_id={"sph": peer}, device_id_type=MESH,
        )
        copy.start()
        copies.append(copy)
    inbox[me] = part[...]
    for copy in copies:
        copy.wait_recv()
    row = jnp.sum(jnp.sum(inbox[...], 0), 0, keepdims=True)
    shift = LANES // 2
    while shift >= dirs:
        row = row + pltpu.roll(row, shift, 1)
        shift //= 2
    total[...] = row
    for copy in copies:
        copy.wait_send()


def sum_all(devices, dirs, part):
    spec = pl.BlockSpec(memory_space=pltpu.VMEM)
    copies = pltpu.SemaphoreType.DMA((devices,))
    return pl.pallas_call(
        functools.partial(sum_kernel, devices, dirs),
        out_shape=jax.ShapeDtypeStruct((1, LANES), jnp.float32),
        in_specs=[spec],
        out_specs=spec,
        scratch_shapes=[pltpu.VMEM((devices,) + part.shape, jnp.float32), copies, copies],
        compiler_params=pltpu.CompilerParams(collective_id=1, has_side_effects=True),
        name="extinction",
    )(part)


def field_kernel(
    dims, lists, table_hbm, mie_sent, phase_rows, pat_rows, pat_tile, mie, cosine, sine,
    scattered, ext, head, chain, phase_at, mie_at, matrix, mixed, acc, table, mie_rows, loaded,
):
    modes, wide, dirs, blocks, classes, step_blocks = dims
    step = pl.program_id(0)
    columns = BLOCK * dirs
    capacity = lists.shape[2]

    load = pltpu.make_async_copy(table_hbm, table, loaded)

    @pl.when(step == 0)
    def _():
        load.start()

        def clear(cell, carry):
            head[cell] = -1
            return carry

        lax.fori_loop(0, blocks * classes, clear, 0)

        def link(device, carry):
            for k in range(capacity):
                cell = lists[device, 0, k]
                slot = device * capacity + k

                @pl.when(cell >= 0)
                def _():
                    chain[slot] = head[cell]
                    head[cell] = slot
                    phase_at[slot] = lists[device, 1, k]
                    mie_at[slot] = lists[device, 2, k]

            return carry

        lax.fori_loop(0, lists.shape[0], link, 0)
        mie_rows[...] = mie_sent[...].astype(jnp.float32)

    def product(slot):
        start = mie_at[slot]
        spread = jnp.broadcast_to(
            phase_rows[pl.ds(phase_at[slot], 1), :], (2 * columns, 2 * columns)
        ).T
        reals, imags = [], []
        for j in range(BLOCK):
            row = mie_rows[pl.ds(start + j, 1), :]
            mr, mi = row[:, :wide], row[:, wide:]
            c = jnp.concatenate([spread[j * dirs : (j + 1) * dirs]] * (wide // LANES), 1)
            s = jnp.concatenate([spread[columns + j * dirs : columns + (j + 1) * dirs]] * (wide // LANES), 1)
            reals.append(c * mr - s * mi)
            imags.append(c * mi + s * mr)
        return jnp.concatenate(reals, 0), jnp.concatenate(imags, 0)

    def build(index, carry):
        kind, local = index // step_blocks, index % step_blocks
        first = head[kind * blocks + step * step_blocks + local]
        rows = pl.ds(pl.multiple_of(local * columns, columns), columns)
        left = pl.ds(pl.multiple_of(kind * 2 * wide, 2 * wide), wide)
        right = pl.ds(pl.multiple_of(kind * 2 * wide + wide, wide), wide)

        @pl.when(first < 0)
        def _():
            zero = jnp.zeros((columns, wide), mixed.dtype)
            mixed[rows, left] = zero
            mixed[rows, right] = zero

        def finish(yr, yi):
            pr, pi = pat_rows[0], pat_rows[1]
            mixed[rows, left] = (yr * pr - yi * pi).astype(mixed.dtype)
            mixed[rows, right] = (yr * pi + yi * pr).astype(mixed.dtype)

        second = chain[jnp.maximum(first, 0)]

        @pl.when((first >= 0) & (second < 0))
        def _():
            finish(*product(first))

        @pl.when((first >= 0) & (second >= 0))
        def _():
            yr, yi = product(first)
            acc[0] = yr
            acc[1] = yi

            def more(slot):
                yr, yi = product(slot)
                acc[0] += yr
                acc[1] += yi
                return chain[slot]

            lax.while_loop(lambda slot: slot >= 0, more, second)
            finish(acc[0], acc[1])

        return carry

    lax.fori_loop(0, classes * step_blocks, build, 0)

    @pl.when(step == 0)
    def _():
        load.wait()
        for kind in range(classes):
            at = kind * 2 * wide
            if wide > modes:
                for part in range(2):
                    end = at + (part + 1) * wide
                    matrix[:, end - LANES : end] = jnp.zeros((2 * modes, LANES), matrix.dtype)
            real, imag = table[kind, 0], table[kind, 1]
            matrix[:modes, at : at + modes] = real
            matrix[:modes, at + wide : at + wide + modes] = -imag
            matrix[modes:, at : at + modes] = imag
            matrix[modes:, at + wide : at + wide + modes] = real

    interaction = lax.dot_general(
        matrix[...], mixed[...], (((1,), (1,)), ((), ())), preferred_element_type=jnp.float32
    )
    width = step_blocks * columns
    per_step = width // dirs
    spheres = mie.shape[1]
    picked = (
        lax.broadcasted_iota(jnp.int32, (spheres, width), 0)
        == step * per_step + lax.broadcasted_iota(jnp.int32, (spheres, width), 1) // dirs
    ).astype(jnp.bfloat16)
    rest, spread_mie = mie[...], 0.0
    for _ in range(3):
        piece = rest.astype(jnp.bfloat16)
        rest = rest - piece.astype(jnp.float32)
        spread_mie += jnp.dot(piece, picked, preferred_element_type=jnp.float32)
    mr, mi = spread_mie[:modes], spread_mie[modes:]
    c, s = cosine[...], sine[...]
    pr = jnp.concatenate([pat_tile[0]] * (width // LANES), 1)
    pi = jnp.concatenate([pat_tile[1]] * (width // LANES), 1)
    inc_r = c * pr - s * pi
    inc_i = c * pi + s * pr
    total_r = inc_r + interaction[:modes]
    total_i = inc_i + interaction[modes:]
    out_r = mr * total_r - mi * total_i
    out_i = mr * total_i + mi * total_r
    scattered[:modes, :] = out_r.astype(scattered.dtype)
    scattered[modes:, :] = out_i.astype(scattered.dtype)
    terms = jnp.sum((inc_r * out_r + inc_i * out_i).reshape(modes // 8, 8, width), 0)
    part = sum(terms[:, at : at + LANES] for at in range(0, width, LANES))

    @pl.when(step == 0)
    def _():
        ext[...] = part

    @pl.when(step > 0)
    def _():
        ext[...] += part


def shards(
    positions, wave_vectors, pattern, dir_index, mie, trans_table, pair_route, pair_source,
    pair_target, pair_class,
):
    modes = pattern.shape[1]
    wide = round_up(modes, LANES)
    spheres = positions.shape[0]
    dirs = dir_index.shape[0]
    columns = BLOCK * dirs
    blocks = spheres // BLOCK
    classes = trans_table.shape[0]
    devices = lax.axis_size("sph")
    me = lax.axis_index("sph")
    pair_count = pair_source.shape[0]
    capacity = max(2, 2 * pair_count // devices)
    slots = devices * capacity
    tables = wave_vectors.shape[0]

    select = (jnp.arange(tables, dtype=jnp.int32)[:, None] == dir_index[None, :]).astype(jnp.float32)
    k = jnp.dot(select.T, wave_vectors, precision=HIGHEST)
    phases = (
        positions[:, 0:1] * k[None, :, 0]
        + positions[:, 1:2] * k[None, :, 1]
        + positions[:, 2:3] * k[None, :, 2]
    )
    cosine, sine = jnp.cos(phases), jnp.sin(phases)
    phase_rows = jnp.concatenate(
        [cosine.reshape(blocks, columns), sine.reshape(blocks, columns)], 1
    )
    dest = pair_route[:, 0]
    order = jnp.arange(pair_count, dtype=jnp.int32)
    rank = jnp.sum(
        ((dest[:, None] == dest[None, :]) & (order[None, :] < order[:, None])).astype(jnp.int32), 1
    )
    slot_of = dest * capacity + rank
    match = slot_of[:, None] == jnp.arange(slots, dtype=jnp.int32)[None, :]
    cell_of = pair_class * blocks + pair_target
    small_rows = round_up(blocks + 3, 8)
    entries = jnp.stack(
        [cell_of + 1, me * small_rows + pair_source, me * spheres + pair_source * BLOCK]
    )
    lists = jnp.sum(jnp.where(match[None], entries[:, :, None], 0), 1)
    lists = (lists - jnp.array([[1], [0], [0]], jnp.int32)).astype(jnp.float32)
    lists = jnp.pad(lists, ((0, small_rows - blocks - 3), (0, LANES - slots)))
    small = jnp.concatenate([phase_rows, lists], 0)
    mie_rows = jnp.pad(jnp.transpose(mie, (2, 0, 1)), ((0, 0), (0, 0), (0, wide - modes)))
    mie_rows = mie_rows.reshape(spheres, 2 * wide).astype(jnp.bfloat16)

    all_mie, all_small = gather_all(devices, mie_rows, small)
    mine = lax.dynamic_slice_in_dim(all_small[:, blocks : blocks + 3], me * capacity, capacity, 2)
    mine = mine.astype(jnp.int32)
    all_mie = all_mie.reshape(devices * spheres, 2 * wide)
    all_small = all_small.reshape(devices * small_rows, LANES)

    select_tile = jnp.concatenate([select] * (LANES // dirs), 1)
    pat_tile = jnp.einsum("cmt,td->cmd", pattern, select_tile, precision=HIGHEST)
    pat_rows = jnp.einsum("td,cmt->cdm", select, pattern, precision=HIGHEST)
    pat_rows = jnp.pad(jnp.concatenate([pat_rows] * BLOCK, 1), ((0, 0), (0, 0), (0, wide - modes)))

    step_blocks = 2 * LANES // columns
    width = step_blocks * columns
    once = pl.Buffered(1)

    def whole(array):
        zeros = (0,) * array.ndim
        return pl.BlockSpec(array.shape, lambda i, *_: zeros, pipeline_mode=once)

    flat_mie = mie.reshape(2 * modes, spheres)
    operands = (trans_table, all_mie, all_small, pat_rows, pat_tile, flat_mie)
    line = pl.BlockSpec((1, width), lambda i, *_: (0, i))
    depth = classes * 2 * wide
    scattered, ext = pl.pallas_call(
        functools.partial(field_kernel, (modes, wide, dirs, blocks, classes, step_blocks)),
        grid_spec=pltpu.PrefetchScalarGridSpec(
            num_scalar_prefetch=1,
            grid=(blocks // step_blocks,),
            in_specs=[pl.BlockSpec(memory_space=pl.ANY)] + [whole(x) for x in operands[1:]] + [line, line],
            out_specs=[
                pl.BlockSpec((2 * modes, width), lambda i, *_: (0, i)),
                pl.BlockSpec((8, LANES), lambda i, *_: (0, 0)),
            ],
            scratch_shapes=[
                pltpu.SMEM((blocks * classes,), jnp.int32),
                pltpu.SMEM((slots,), jnp.int32),
                pltpu.SMEM((slots,), jnp.int32),
                pltpu.SMEM((slots,), jnp.int32),
                pltpu.VMEM((2 * modes, depth), jnp.bfloat16),
                pltpu.VMEM((width, depth), jnp.bfloat16),
                pltpu.VMEM((2, columns, wide), jnp.float32),
                pltpu.VMEM(trans_table.shape, jnp.bfloat16),
                pltpu.VMEM(all_mie.shape, jnp.float32),
                pltpu.SemaphoreType.DMA(()),
            ],
        ),
        out_shape=[
            jax.ShapeDtypeStruct((2 * modes, spheres * dirs), jnp.bfloat16),
            jax.ShapeDtypeStruct((8, LANES), jnp.float32),
        ],
        compiler_params=pltpu.CompilerParams(
            dimension_semantics=("arbitrary",), vmem_limit_bytes=60 * 1024 * 1024
        ),
        name="field",
    )(mine, *operands, cosine.reshape(1, spheres * dirs), sine.reshape(1, spheres * dirs))
    return (scattered, sum_all(devices, dirs, ext)[0, :dirs])


def solution(mesh):
    placed = (
        P("sph", None), P(), P(), P("groups"), P(None, None, "sph"), P(),
        P("sph", None), P("sph"), P("sph"), P("sph"),
    )
    return jax.shard_map(
        shards,
        mesh=mesh,
        in_specs=placed,
        out_specs=(P(None, ("groups", "sph")), P("groups")),
        check_vma=False,
    )
```
